256 devices in a mesh: depth: 8 (over x, y_lo), lat: 32 (over y_hi, z, core).
Axes of the slice: x: 4, y: 4 (y_hi: 2, y_lo: 2; y = y_hi * 2 + y_lo), z: 8, core: 2. Of those that a mesh axis runs over, the one named last changes fastest.
Arguments:
- probe: bfloat16 [2, 256, 256], replicated, may hold values from -6 to 6
- positions: int32 [2, 128, 2], P(None, 'lat'), may hold values from 0 to 255
- object_phase: bfloat16 [8, 8192, 512], P('depth', 'lat'), may hold values from -3.140625 to 3.140625
- propagator: float32 [256, 256], replicated, may hold values from -3.140625 to 3.140625
- stored: bfloat16 [8, 128, 2, 256, 256], P('depth', 'lat'), may hold values from -6 to 6
- measured: float32 [128, 256, 256], P('lat'), may hold values from 0 to 2
Outputs:
- leaving: bfloat16 [8, 128, 2, 256, 256], P('depth', 'lat')
- gradient: float32 [8, 2, 8192, 512], P('depth', None, 'lat')
The draws below stay inside these ranges and needn't reach their ends.
Inputs may be any that keep to these rules, and one draw needn't show every extreme that they name: positions[d, q, 0] and positions[d, q, 1] are the row and column of the corner of probe q's window inside the tile of probe q; windows reach into the next tile's first rows.
All inputs are finite; a program needn't handle non-finite values.
Results may differ from the reference program's by a relative error of at most 0.04.
Values may be sent and summed in bfloat16 or wider, within the bound.
No kernel may reach another device: no remote copies, remote signals or barrier semaphores. Data moves between devices by JAX's collectives and lax.ppermute only.
A program may use at most 64 MiB of HBM per device.

```python
import math
import jax
import jax.numpy as jnp
from jax import lax

NPIX = 256
SLICES = 1
TX = 256
PROBES = 4
COLS = 512
ROWS = 8192
LAYERS = 8
PROBES_ALL = 128
N_DEPTH = 8


def place_ends(array, own_key, smallest, largest):
    shape = array.shape
    spot = [jax.random.randint(jax.random.fold_in(own_key, axis), (), 0, shape[axis]) for axis in range(len(shape))]
    array = array.at[tuple(spot)].set(smallest)
    longest = shape.index(max(shape))
    spot[longest] = (spot[longest] + 1) % shape[longest]
    return array.at[tuple(spot)].set(largest)


def level_of(own_key, dims, split, least, largest):
    loudness = 1.0
    for axis_at, shards_of in split:
        heights = jax.random.uniform(jax.random.fold_in(jax.random.fold_in(own_key, 6), axis_at), (shards_of,), jnp.float32, least / len(split), largest / len(split))
        loudness = loudness * jnp.repeat(jnp.exp(heights), dims[axis_at] // shards_of).reshape((-1,) + (1,) * (len(dims) - 1 - axis_at))
    return loudness


def scatter_about(stream_key, extent, scale, limit, shards=(), kind=jnp.bfloat16):
    values = jax.random.normal(stream_key, extent, jnp.float32) * scale
    if len(shards) > 0:
        values = level_of(stream_key, extent, shards, -0.22, 0.18) * values
    return jnp.clip(values, min=-limit, max=limit).astype(kind)


def setup_inputs(seed: int = 0) -> dict:
    keys = jax.random.split(jax.random.key(seed), 7)
    probe = scatter_about(keys[0], (2, NPIX, NPIX), 1.0, 6.0)
    positions = place_ends(jax.random.randint(keys[1], (2, PROBES_ALL, 2), 0, TX), jax.random.fold_in(keys[1], 1), 0, TX - 1).astype(jnp.int32)
    object_phase = jnp.clip(jax.random.uniform(keys[2], (LAYERS, ROWS, COLS), jnp.float32, -3.140625, 3.140625), -3.140625, 3.140625).astype(jnp.bfloat16)
    propagator = jnp.clip(jax.random.uniform(keys[3], (NPIX, NPIX), jnp.float32, -3.140625, 3.140625), -3.140625, 3.140625)
    stored = scatter_about(keys[4], (N_DEPTH, PROBES_ALL, 2, NPIX, NPIX), 1.0, 6.0, ((0, 8), (1, 32)))
    measured = jnp.clip(2.0 * jax.random.uniform(keys[5], (PROBES_ALL, NPIX, NPIX), jnp.float32) ** level_of(keys[5], (PROBES_ALL, NPIX, NPIX), ((0, 32),), -0.2, 0.2), 0.0, 2.0)
    return dict(probe=probe, positions=positions, object_phase=object_phase, propagator=propagator, stored=stored, measured=measured)


def tables():
    counter = jnp.arange(NPIX, dtype=jnp.int32)
    product = counter[:, None] * counter[None, :] % NPIX
    angles = 2.0 * math.pi / NPIX * product.astype(jnp.float32)
    factor = 1.0 / math.sqrt(NPIX)
    real_part = jnp.cos(angles) * factor
    imag_part = -jnp.sin(angles) * factor
    forward = jnp.stack([jnp.stack([real_part, -imag_part]), jnp.stack([imag_part, real_part])]).astype(jnp.bfloat16)
    inverse = jnp.stack([jnp.stack([real_part, imag_part]), jnp.stack([-imag_part, real_part])]).astype(jnp.bfloat16)
    return (forward, inverse)

def transform(table, waves):
    left = jnp.einsum('abjk,pbkl->pajl', table.astype(jnp.float32), waves.astype(jnp.float32)).astype(jnp.bfloat16)
    return jnp.einsum('pbjk,abkl->pajl', left.astype(jnp.float32), table.astype(jnp.float32))

def times(first, second):
    first = first.astype(jnp.float32)
    second = second.astype(jnp.float32)
    real_part = first[..., 0, :, :] * second[..., 0, :, :] - first[..., 1, :, :] * second[..., 1, :, :]
    imag_part = first[..., 0, :, :] * second[..., 1, :, :] + first[..., 1, :, :] * second[..., 0, :, :]
    return jnp.stack([real_part, imag_part], axis=-3)

def conj_times(first, second):
    first = first.astype(jnp.float32)
    second = second.astype(jnp.float32)
    real_part = first[..., 0, :, :] * second[..., 0, :, :] + first[..., 1, :, :] * second[..., 1, :, :]
    imag_part = first[..., 0, :, :] * second[..., 1, :, :] - first[..., 1, :, :] * second[..., 0, :, :]
    return jnp.stack([real_part, imag_part], axis=-3)

def slice_forward(wave, transmit, kernel, forward, inverse):
    exited = times(wave, transmit).astype(jnp.bfloat16)
    spectrum = transform(forward, exited)
    shifted = times(kernel, spectrum).astype(jnp.bfloat16)
    return transform(inverse, shifted).astype(jnp.bfloat16)

def slice_adjoint(adjoint, wave, transmit, kernel, forward, inverse):
    spectrum = transform(forward, adjoint)
    shifted = conj_times(kernel, spectrum).astype(jnp.bfloat16)
    exited = transform(inverse, shifted)
    term = conj_times(wave, exited)
    return (conj_times(transmit, exited).astype(jnp.bfloat16), term)

def far_adjoint(exit_wave, intensity, forward, inverse):
    field = transform(forward, exit_wave)
    power = field[..., 0, :, :] * field[..., 0, :, :] + field[..., 1, :, :] * field[..., 1, :, :]
    weight = (power - intensity)[..., None, :, :] * field
    return transform(inverse, weight.astype(jnp.bfloat16)).astype(jnp.bfloat16)

def windows(layer_phase, rows, cols):

    def single(row, col):
        return lax.dynamic_slice(layer_phase, (row, col), (NPIX, NPIX))
    cut = jax.vmap(single)(rows, cols).astype(jnp.float32)
    return jnp.stack([jnp.cos(cut), jnp.sin(cut)], axis=1)

def reference(probe, positions, object_phase, propagator, stored, measured):
    forward, inverse = tables()
    kernel = jnp.stack([jnp.cos(propagator), jnp.sin(propagator)])
    owner = jnp.arange(PROBES_ALL, dtype=jnp.int32) // PROBES
    ahead_rows = (owner * TX + positions[0, :, 0]).astype(jnp.int32)
    ahead_cols = positions[0, :, 1].astype(jnp.int32)
    behind_rows = (owner * TX + positions[1, :, 0]).astype(jnp.int32)
    behind_cols = positions[1, :, 1].astype(jnp.int32)
    extended = jnp.concatenate([object_phase, object_phase[:, :NPIX]], axis=1)
    sections = extended.reshape(N_DEPTH, SLICES, ROWS + NPIX, COLS)

    def ahead(wave, layers):
        for index in range(SLICES):
            wave = slice_forward(wave, windows(layers[index], ahead_rows, ahead_cols), kernel, forward, inverse)
        return (wave, wave)
    start = jnp.broadcast_to(probe, (PROBES_ALL, 2, NPIX, NPIX))
    _, leaving = lax.scan(ahead, start, sections)

    def replay(wave, layers):
        inputs = []
        transmits = []
        for index in range(SLICES):
            transmit = windows(layers[index], behind_rows, behind_cols)
            inputs.append(wave)
            transmits.append(transmit)
            wave = slice_forward(wave, transmit, kernel, forward, inverse)
        return (wave, inputs, transmits)
    last_exit, _, _ = replay(stored[N_DEPTH - 1], sections[N_DEPTH - 1])
    adjoint = far_adjoint(last_exit, measured, forward, inverse)

    def behind(adjoint, pair):
        layers, start_wave = pair
        _, inputs, transmits = replay(start_wave, layers)
        terms = [None] * SLICES
        for index in reversed(range(SLICES)):
            adjoint, terms[index] = slice_adjoint(adjoint, inputs[index], transmits[index], kernel, forward, inverse)
        return (adjoint, jnp.stack(terms))
    _, terms = lax.scan(behind, adjoint, (sections, stored), reverse=True)
    terms = terms.reshape(LAYERS, PROBES_ALL, 2, NPIX, NPIX)
    gradient = jnp.zeros((LAYERS, 2, ROWS + NPIX, COLS), jnp.float32)
    anchor = jnp.zeros((), jnp.int32)

    def place(probe_index, gradient):
        corner = (anchor, anchor, behind_rows[probe_index], behind_cols[probe_index])
        piece = lax.dynamic_slice(gradient, corner, (LAYERS, 2, NPIX, NPIX))
        piece = piece + lax.dynamic_index_in_dim(terms, probe_index, 1, False)
        return lax.dynamic_update_slice(gradient, piece, corner)
    gradient = lax.fori_loop(0, PROBES_ALL, place, gradient)
    folded = gradient[:, :, :ROWS].at[:, :, :NPIX].add(gradient[:, :, ROWS:])
    return (leaving, folded)
```

```python
import jax
import jax.numpy as jnp
import numpy as np
from jax import lax
from jax.experimental import pallas as pl
from jax.experimental.pallas import tpu as pltpu
from jax.sharding import PartitionSpec as P


def fit(function, degrees, limit):
    points = limit * np.cos((np.arange(400) + 0.5) * np.pi / 400)
    basis = np.stack([points**degree for degree in degrees], 1)
    return np.linalg.lstsq(basis, function(points), rcond=None)[0]


SIN = [float(value) for value in fit(np.sin, (1, 3, 5, 7, 9), 1.571)]
COS = [float(value) for value in fit(np.cos, (0, 2, 4, 6, 8, 10), 1.571)]


def horner(coefficients, x):
    total = coefficients[-1]
    for value in coefficients[-2::-1]:
        total = total * x + value
    return total


def cis(phase):
    half = phase * 0.5
    square = half * half
    sine = horner(SIN, square) * half
    cosine = horner(COS, square)
    double = sine + sine
    return 1.0 - double * sine, double * cosine


def tables(npix):
    counter = np.arange(npix)
    angles = 2.0 * np.pi / npix * (counter[:, None] * counter[None, :] % npix)
    real_part = (np.cos(angles) / np.sqrt(npix)).astype(np.float32)
    imag_part = (-np.sin(angles) / np.sqrt(npix)).astype(np.float32)
    left = np.block([[real_part, -imag_part], [imag_part, real_part]])
    right = np.block([[real_part, imag_part], [-imag_part, real_part]])
    return jnp.asarray(left, jnp.bfloat16), jnp.asarray(right, jnp.bfloat16)


def dot(first, second):
    return jnp.dot(first, second, preferred_element_type=jnp.float32)


def transform(real, imag, left, right):
    npix = real.shape[0]
    half = dot(left, jnp.concatenate([real, imag], 0)).astype(jnp.bfloat16)
    full = dot(jnp.concatenate([half[:npix], half[npix:]], 1), right)
    return full[:, :npix], full[:, npix:]


def times(a, b, c, d):
    return a * c - b * d, a * d + b * c


def conj_times(a, b, c, d):
    return a * c + b * d, a * d - b * c


def narrow(pair):
    return pair[0].astype(jnp.bfloat16), pair[1].astype(jnp.bfloat16)


def wide(pair):
    return pair[0].astype(jnp.float32), pair[1].astype(jnp.float32)


def cut_kernel(positions, tile, edge, out, extended):
    rows, columns = tile.shape
    npix = out.shape[-1]
    extended[:rows] = tile[...].astype(jnp.float32)
    extended[rows:] = edge[...].astype(jnp.float32)

    def step(index, carry):
        direction, probe = index // 4, index % 4
        row = positions[direction, probe, 0]
        column = positions[direction, probe, 1]
        start = pl.multiple_of(row // 8 * 8, 8)
        strip = extended[pl.ds(start, npix + 8), :]
        strip = pltpu.roll(strip, lax.rem(columns - column, columns), 1)[:, :npix]
        strip = pltpu.roll(strip, lax.rem(npix + 8 - lax.rem(row, 8), npix + 8), 0)
        out[index] = strip[:npix].astype(out.dtype)
        return carry

    lax.fori_loop(0, 8, step, 0)


def chain_kernel(
    place, windows, probe, stored, sent_0, sent_1, sent_2, measured, propagator, left, right, out, shift, wave
):
    device = place[0]
    layers = windows.shape[0]
    shift[0], shift[1] = cis(propagator[...])

    def forward(pair):
        return transform(*pair, left[...], right[...])

    def inverse(pair):
        return transform(*pair, right[...], left[...])

    def advance(pair, layer):
        transmit = cis(windows[layer].astype(jnp.float32))
        exited = narrow(times(*wide(pair), *transmit))
        moved = narrow(times(shift[0], shift[1], *forward(exited)))
        return narrow(inverse(moved))

    @pl.when(device < 4)
    def _():
        wave[...] = probe[...]

        def step(layer, carry):
            pair = advance((wave[0], wave[1]), layer)
            wave[0], wave[1] = pair
            out[layer, 0], out[layer, 1] = pair
            return carry

        lax.fori_loop(0, layers, step, 0)

    @pl.when(device >= 4)
    def _():
        for index, sent in enumerate((sent_0, sent_1, sent_2)):

            @pl.when(device == 4 + index)
            def _():
                wave[...] = sent[...]

        @pl.when(device == 7)
        def _():
            wave[...] = stored[0, 3]

        exit_wave = advance((wave[0], wave[1]), layers - 1)
        real, imag = forward(exit_wave)
        weight = real * real + imag * imag - measured[device - 4]
        wave[0], wave[1] = narrow(inverse(narrow((weight * real, weight * imag))))

        def step(index, carry):
            layer = layers - 1 - index
            moved = narrow(conj_times(shift[0], shift[1], *forward((wave[0], wave[1]))))
            exited = inverse(moved)
            out[layer, 0], out[layer, 1] = narrow(exited)
            transmit = cis(windows[layer].astype(jnp.float32))
            wave[0], wave[1] = narrow(conj_times(*transmit, *exited))
            return carry

        lax.fori_loop(0, layers, step, 0)


def place_kernel(positions, back, stored, leaving, own, rim, total):
    rows, columns = own.shape[1:]
    npix = back.shape[-1]
    leaving[0] = back[:4]
    total[...] = jnp.zeros_like(total)

    def step(probe, carry):
        row = positions[1, probe, 0]
        column = positions[1, probe, 1]
        start = pl.multiple_of(row // 8 * 8, 8)
        pair = conj_times(
            stored[0, probe, 0].astype(jnp.float32),
            stored[0, probe, 1].astype(jnp.float32),
            back[4 + probe, 0].astype(jnp.float32),
            back[4 + probe, 1].astype(jnp.float32),
        )
        for part in range(2):
            padded = jnp.concatenate([pair[part], jnp.zeros((8, npix), jnp.float32)], 0)
            padded = pltpu.roll(padded, lax.rem(row, 8), 0)
            padded = jnp.concatenate([padded, jnp.zeros_like(padded)], 1)
            total[part, pl.ds(start, npix + 8), :] += pltpu.roll(padded, column, 1)
        return carry

    lax.fori_loop(0, 4, step, 0)
    own[...] = total[:, :rows]
    rim[...] = total[:, rows:].astype(rim.dtype)


VMEM = pl.BlockSpec(memory_space=pltpu.VMEM)
SMEM = pl.BlockSpec(memory_space=pltpu.SMEM)
PARAMS = pltpu.CompilerParams(vmem_limit_bytes=40 << 20)


def body(probe, positions, object_phase, propagator, stored, measured):
    npix = probe.shape[-1]
    _, rows, columns = object_phase.shape
    tiles = lax.axis_size("lat")
    depth = lax.axis_size("depth")
    left, right = tables(npix)
    tile = object_phase[0]
    edge = lax.ppermute(tile, "lat", [(i, (i - 1) % tiles) for i in range(tiles)])
    sent = [lax.ppermute(stored[0, i], "depth", [(depth - 1, 4 + i)]) for i in range(3)]
    windows = pl.pallas_call(
        cut_kernel,
        out_shape=jax.ShapeDtypeStruct((8, npix, npix), jnp.bfloat16),
        in_specs=[SMEM, VMEM, VMEM],
        out_specs=VMEM,
        scratch_shapes=[pltpu.VMEM((rows + npix, columns), jnp.float32)],
        compiler_params=PARAMS,
        name="cut",
    )(positions, tile, edge)
    windows = lax.all_to_all(windows, "depth", 0, 0, tiled=True)
    place = lax.axis_index("depth").astype(jnp.int32).reshape(1)
    results = pl.pallas_call(
        chain_kernel,
        out_shape=jax.ShapeDtypeStruct((depth, 2, npix, npix), jnp.bfloat16),
        in_specs=[SMEM] + [VMEM] * 10,
        out_specs=VMEM,
        scratch_shapes=[pltpu.VMEM((2, npix, npix), jnp.float32), pltpu.VMEM((2, npix, npix), jnp.bfloat16)],
        compiler_params=PARAMS,
        name="chain",
    )(place, windows, probe, stored, *sent, measured, propagator, left, right)
    back = lax.all_to_all(results, "depth", 0, 0, tiled=True)
    leaving, own, rim = pl.pallas_call(
        place_kernel,
        out_shape=(
            jax.ShapeDtypeStruct((1, 4, 2, npix, npix), jnp.bfloat16),
            jax.ShapeDtypeStruct((2, rows, columns), jnp.float32),
            jax.ShapeDtypeStruct((2, npix, columns), jnp.bfloat16),
        ),
        in_specs=[SMEM, VMEM, VMEM],
        out_specs=(VMEM, VMEM, VMEM),
        scratch_shapes=[pltpu.VMEM((2, rows + npix, columns), jnp.float32)],
        compiler_params=PARAMS,
        name="place",
    )(positions, back, stored)
    rim = lax.ppermute(rim, "lat", [(i, (i + 1) % tiles) for i in range(tiles)])
    gradient = own + rim.astype(jnp.float32)
    return leaving, gradient[None]


def solution(mesh):
    return jax.shard_map(
        body,
        mesh=mesh,
        in_specs=(
            P(),
            P(None, "lat", None),
            P("depth", "lat", None),
            P(),
            P("depth", "lat", None, None, None),
            P("lat", None, None),
        ),
        out_specs=(P("depth", "lat", None, None, None), P("depth", None, "lat", None)),
        check_vma=False,
    )
```
